32 devices in a mesh: dp: 4 (over x, core), tensor: 8 (over z, y).
Axes of the slice: x: 2, y: 2, z: 4, core: 2. Of those that a mesh axis runs over, the one named last changes fastest.
Arguments:
- tokens: bfloat16 [2, 2048, 4, 1024], P(None, 'tensor', 'dp'), may hold values from -6 to 6
- cotangent: bfloat16 [2, 2048, 4, 1024], P(None, 'tensor', 'dp'), may hold values from -6 to 6
- timesteps: int32 [2, 4, 2], P(None, 'dp'), may hold values from 0 to 999
- bucket: int32 [2, 4], P(None, 'dp'), may hold values 0 or 1
- counts: int32 [2, 4], P(None, 'dp'), may hold values from 8 to 48, as said below
- qkv_weight: bfloat16 [3, 1024, 1024], P(None, None, 'tensor'), may hold values from -0.1875 to 0.1875
- qv_bias: float32 [2, 1024], P(None, 'tensor'), may hold values from -3 to 3
- out_weight: bfloat16 [1024, 1024], P('tensor'), may hold values from -2 to 2
- out_bias: float32 [1024], replicated, may hold values from -2 to 2
- norm1_gain: float32 [1024], replicated, may hold values from 0.25 to 1.75
- norm1_bias: float32 [1024], replicated, may hold values from -2 to 2
- up_weight: bfloat16 [1024, 4096], P(None, 'tensor'), may hold values from -0.1875 to 0.1875
- up_bias: float32 [4096], P('tensor'), may hold values from -3 to 3
- down_weight: bfloat16 [4096, 1024], P('tensor'), may hold values from -0.09375 to 0.09375
- down_bias: float32 [1024], replicated, may hold values from -2 to 2
- norm2_gain: float32 [1024], replicated, may hold values from 0.25 to 1.75
- norm2_bias: float32 [1024], replicated, may hold values from -2 to 2
Outputs:
- layer_out: bfloat16 [2, 2048, 4, 1024], P(None, 'tensor', 'dp')
- tokens_grad: float32 [2, 2048, 4, 1024], P(None, 'tensor', 'dp')
- qkv_grad: float32 [3, 1024, 1024], P(None, 'dp', 'tensor')
- qv_bias_grad: float32 [2, 1024], P(None, ('tensor', 'dp'))
- out_weight_grad: float32 [1024, 1024], P('tensor', 'dp')
- up_weight_grad: float32 [1024, 4096], P('dp', 'tensor')
- up_bias_grad: float32 [4096], P(('tensor', 'dp'))
- down_weight_grad: float32 [4096, 1024], P('tensor', 'dp')
- vector_grads: float32 [6, 1024], P(None, ('dp', 'tensor'))
The draws below stay inside these ranges and needn't reach their ends.
Inputs may be any that keep to these rules, and one draw needn't show every extreme that they name: True counts are positive.
All inputs are finite; a program needn't handle non-finite values. No bound on the sum of `bucket` on one device may be relied on, other than what follows from the above.
Results may differ from the reference program's by a relative error of at most 0.02.
Values may be sent and summed in bfloat16 or wider, within the bound.
A program may use at most 320 MiB of HBM per device.

```python
import math
import jax
import jax.numpy as jnp
from jax import lax

HEADS = 16
HD = 64
FF = 4096
D = 1024
SEQ = 2048
MICRO = 2
ITEMS_MB = 1
ITEMS = 4


def draw_counts(key, part):
    base_count = jax.random.randint(key, (MICRO, ITEMS), 8, 17)
    base_count = base_count.at[0, 0].set(8).at[0, ITEMS - 1].set(16)
    groups = ITEMS // ITEMS_MB
    group_index = jnp.arange(ITEMS) // ITEMS_MB
    return (base_count * (groups - 1 + 2 * group_index)[None, :] // (groups - 1)).astype(jnp.int32)


def set_ends(array, key, smallest, high):
    spot = [jax.random.randint(jax.random.fold_in(key, axis), (), 0, length) for axis, length in enumerate(array.shape)]
    widest = array.shape.index(max(array.shape))
    beside = spot[:widest] + [(spot[widest] + 1) % array.shape[widest]] + spot[widest + 1:]
    return array.at[tuple(spot)].set(smallest).at[tuple(beside)].set(high)


def steps_of(stream_key, dims, cuts, smallest, largest):
    level = 1.0
    for dim, blocks in cuts:
        steps = jax.random.uniform(jax.random.fold_in(jax.random.fold_in(stream_key, 6), dim), (blocks,), jnp.float32, smallest / len(cuts), largest / len(cuts))
        level = level * jnp.repeat(jnp.exp(steps), dims[dim] // blocks).reshape((-1,) + (1,) * (len(dims) - 1 - dim))
    return level


def gaussian(key, shape, scale, most, split=(), held_as=jnp.bfloat16):
    entries = scale * jax.random.normal(key, shape, jnp.float32)
    if split:
        entries = entries * steps_of(key, shape, split, -0.22, 0.18)
    return jnp.clip(entries, -most, most).astype(held_as)


def setup_inputs(seed: int = 0) -> dict:
    arg_keys = jax.random.split(jax.random.key(seed), 18)
    tokens = gaussian(arg_keys[0], (MICRO, SEQ, ITEMS, D), 1.0, 6.0, ((1, 8), (2, 4)))
    cotangent = gaussian(arg_keys[1], (MICRO, SEQ, ITEMS, D), 1.0, 6.0, ((1, 8), (2, 4)))
    timesteps = set_ends(jax.random.randint(arg_keys[2], (MICRO, ITEMS, 2), 0, 1000), jax.random.fold_in(arg_keys[2], 1), 0, 999).astype(jnp.int32)
    bucket = set_ends((jax.random.randint(arg_keys[3], (MICRO, ITEMS), 0, 4) < 3).astype(jnp.int32), jax.random.fold_in(arg_keys[3], 1), 0, 1)
    counts = draw_counts(jax.random.fold_in(arg_keys[17], 71), 0)
    qkv_weight = gaussian(arg_keys[5], (3, D, D), D ** -0.5, 0.1875, ((2, 8),))
    qv_bias = gaussian(arg_keys[6], (2, D), 0.5, 3.0, ((1, 8),), jnp.float32)
    out_weight = gaussian(arg_keys[7], (D, D), (max(D // 128, 4)) ** -0.5, 2.0, ((0, 8),))
    out_bias = gaussian(arg_keys[8], (D,), 0.3, 2.0, (), jnp.float32)
    norm1_gain = jnp.clip(1.0 + 0.15 * jax.random.normal(arg_keys[9], (D,), jnp.float32), 0.25, 1.75)
    norm1_bias = gaussian(arg_keys[10], (D,), 0.3, 2.0, (), jnp.float32)
    up_weight = gaussian(arg_keys[11], (D, FF), D ** -0.5, 0.1875, ((1, 8),))
    up_bias = gaussian(arg_keys[12], (FF,), 0.5, 3.0, ((0, 8),), jnp.float32)
    down_weight = gaussian(arg_keys[13], (FF, D), FF ** -0.5, 0.09375, ((0, 8),))
    down_bias = gaussian(arg_keys[14], (D,), 0.3, 2.0, (), jnp.float32)
    norm2_gain = jnp.clip(1.0 + 0.15 * jax.random.normal(arg_keys[15], (D,), jnp.float32), 0.25, 1.75)
    norm2_bias = gaussian(arg_keys[16], (D,), 0.3, 2.0, (), jnp.float32)
    return dict(tokens=tokens, cotangent=cotangent, timesteps=timesteps, bucket=bucket, counts=counts, qkv_weight=qkv_weight, qv_bias=qv_bias, out_weight=out_weight, out_bias=out_bias, norm1_gain=norm1_gain, norm1_bias=norm1_bias, up_weight=up_weight, up_bias=up_bias, down_weight=down_weight, down_bias=down_bias, norm2_gain=norm2_gain, norm2_bias=norm2_bias)


EPS = 1e-05

@jax.custom_vjp
def low(v):
    return lax.optimization_barrier(v.astype(jnp.bfloat16)).astype(jnp.float32)

@jax.custom_vjp
def low_back(v):
    return v

def low_keep(v):
    return (low(v), None)

def low_pass(kept, grad):
    return (grad,)

def back_keep(v):
    return (v, None)

def back_low(kept, grad):
    return (low(grad),)
low.defvjp(low_keep, low_pass)
low_back.defvjp(back_keep, back_low)

def matmul_high(left, right):
    return jnp.dot(left, right, precision=lax.Precision.HIGHEST, preferred_element_type=jnp.float32)

def sinusoid(steps):
    half_width = D // 2
    freqs = jnp.exp(jnp.arange(half_width).astype(jnp.float32) * (-2.0 * math.log(10000.0) / D))
    angles = steps.astype(jnp.float32)[..., None] * freqs
    return jnp.concatenate([jnp.sin(angles), jnp.cos(angles)], axis=-1)

def layer_norm(values, gain, shift):
    average = lax.optimization_barrier(jnp.mean(values, axis=-1, keepdims=True))
    centred = values - average
    spread = lax.optimization_barrier(jnp.mean(centred * centred, axis=-1, keepdims=True))
    return centred * lax.rsqrt(spread + EPS) * gain + shift

def attend(queries, keys, values):
    scale = float(HD) ** (-0.5)
    scores = low_back(jnp.einsum('qhd,khd->hqk', queries, keys, precision=lax.Precision.HIGHEST) * scale)
    probs = low(jax.nn.softmax(scores, axis=-1))
    return jnp.einsum('hqk,khd->qhd', probs, values, precision=lax.Precision.HIGHEST)

def forward(params, inputs, temb):
    qkv_w, qv_b, out_w, out_b, gain_one, shift_one, up_w, up_b, down_w, down_b, gain_two, shift_two = params
    hidden = inputs + temb
    hidden_low = low(hidden)
    queries = low(low_back(matmul_high(hidden_low, qkv_w[0]) + qv_b[0])).reshape(SEQ, HEADS, HD)
    keys = low(low_back(matmul_high(hidden_low, qkv_w[1]))).reshape(SEQ, HEADS, HD)
    values = low(low_back(matmul_high(hidden_low, qkv_w[2]) + qv_b[1])).reshape(SEQ, HEADS, HD)
    half_len = SEQ // 2
    pieces = []
    for block in range(2):
        limit = (block + 1) * half_len
        pieces.append(jax.checkpoint(attend)(queries[block * half_len:limit], keys[:limit], values[:limit]))
    context = low(low_back(jnp.concatenate(pieces, axis=0).reshape(SEQ, D)))
    attention = low_back(matmul_high(context, out_w)) + out_b
    normed = layer_norm(hidden + attention, gain_one, shift_one)
    normed_low = low(normed)
    pre = low_back(matmul_high(normed_low, up_w) + up_b)
    act = low(jax.nn.gelu(pre, approximate=False))
    branch = low_back(matmul_high(act, down_w)) + down_b
    return layer_norm(normed + branch, gain_two, shift_two)

def reference(tokens, cotangent, timesteps, bucket, counts, qkv_weight, qv_bias, out_weight, out_bias, norm1_gain, norm1_bias, up_weight, up_bias, down_weight, down_bias, norm2_gain, norm2_bias):
    params = (qkv_weight.astype(jnp.float32), qv_bias, out_weight.astype(jnp.float32), out_bias, norm1_gain, norm1_bias, up_weight.astype(jnp.float32), up_bias, down_weight.astype(jnp.float32), down_bias, norm2_gain, norm2_bias)
    total_items = MICRO * ITEMS
    inputs = tokens.astype(jnp.float32).transpose(0, 2, 1, 3).reshape(total_items, SEQ, D)
    grads_in = cotangent.astype(jnp.float32).transpose(0, 2, 1, 3).reshape(total_items, SEQ, D)
    steps_all = timesteps.reshape(total_items, 2)
    count_f = counts.astype(jnp.float32).reshape(total_items)
    total = jnp.sum(count_f)
    weights = count_f * float(total_items) / total
    late = jnp.arange(SEQ) >= SEQ // 2
    live = jnp.where(late[None, :], bucket.reshape(total_items)[:, None], 1).astype(jnp.float32)

    def step(carry, item):
        inputs_one, grads_one, steps_one, weight_one, live_one = item
        embedded = sinusoid(steps_one)
        temb = jnp.where(late[:, None], embedded[1][None, :], embedded[0][None, :])
        result, pullback = jax.vjp(lambda param_set, input_set: forward(param_set, input_set, temb), params, inputs_one)
        cotan = grads_one * weight_one * live_one[:, None]
        grad_params, grad_inputs = pullback(cotan)
        carry = jax.tree.map(lambda running, addend: running + addend, carry, grad_params)
        return (carry, (result, grad_inputs))
    zeros = jax.tree.map(jnp.zeros_like, params)
    finals, (outputs, input_grads) = lax.scan(step, zeros, (inputs, grads_in, steps_all, weights, live))
    layer_out = outputs.reshape(MICRO, ITEMS, SEQ, D).transpose(0, 2, 1, 3).astype(jnp.bfloat16)
    tokens_grad = input_grads.reshape(MICRO, ITEMS, SEQ, D).transpose(0, 2, 1, 3)
    vector_grads = jnp.stack([finals[3], finals[4], finals[5], finals[9], finals[10], finals[11]])
    return (layer_out, tokens_grad, finals[0], finals[1], finals[2], finals[6], finals[7], finals[8], vector_grads)
```

```python
import math

import jax
import jax.numpy as jnp
from jax import lax
from jax.sharding import PartitionSpec as P

HD = 64


EPS = 1e-05
INV_ROOT_TWO = 1.0 / math.sqrt(2.0)
INV_ROOT_TWO_PI = 1.0 / math.sqrt(2.0 * math.pi)


def sinusoid(steps, width):
    half_width = width // 2
    freqs = jnp.exp(jnp.arange(half_width).astype(jnp.float32) * (-2.0 * math.log(10000.0) / width))
    angles = steps.astype(jnp.float32)[..., None] * freqs
    return jnp.concatenate([jnp.sin(angles), jnp.cos(angles)], axis=-1)


def norm_forward(values, gain, shift):
    average = jnp.mean(values, axis=-1, keepdims=True)
    centred = values - average
    spread = jnp.mean(centred * centred, axis=-1, keepdims=True)
    inverse = lax.rsqrt(spread + EPS)
    unit = centred * inverse
    return (unit * gain + shift, unit, inverse)


def norm_backward(grad, unit, inverse, gain):
    scaled = grad * gain
    first = jnp.mean(scaled, axis=-1, keepdims=True)
    second = jnp.mean(scaled * unit, axis=-1, keepdims=True)
    return inverse * (scaled - first - unit * second)


SLOTS = (0, 4, 2, 6, 1, 5, 3, 7)


class Plain:
    def __init__(self):
        self.parts = lax.axis_size("tensor")

    def sum_dp(self, value):
        return lax.psum(value, "dp")

    def gather(self, shard, x_first=False):
        return lax.all_gather(shard, "tensor", axis=0, tiled=False)

    def gather_bias(self, shard):
        return lax.all_gather(shard, "tensor", axis=0, tiled=False)

    def columns(self, array):
        return array

    def scatter(self, grads, x_first=False):
        part = lax.psum_scatter(grads, "tensor", scatter_dimension=0, tiled=True)[0]
        return lax.psum_scatter(part, "dp", scatter_dimension=1, tiled=True)

    def scatter_bias(self, grads):
        part = lax.psum_scatter(grads, "tensor", scatter_dimension=0, tiled=True)[0]
        return lax.psum_scatter(part, "dp", scatter_dimension=0, tiled=True)

    def scatter_vectors(self, vectors):
        return lax.psum_scatter(vectors, ("dp", "tensor"), scatter_dimension=1, tiled=True)

    def scatter_qkv(self, grads):
        return lax.psum_scatter(grads, "dp", scatter_dimension=1, tiled=True)

    def scatter_qv(self, grads):
        return lax.psum_scatter(grads, "dp", scatter_dimension=1, tiled=True)

    def to_tokens(self, context):
        seq = context.shape[0]
        split = context.reshape((self.parts, seq // self.parts) + context.shape[1:])
        return lax.all_to_all(split, "tensor", 0, 0, tiled=True)

    def to_heads(self, blocks):
        moved = lax.all_to_all(blocks, "tensor", 0, 0, tiled=True)
        return moved.reshape((-1,) + moved.shape[2:])


class Cube(Plain):
    def __init__(self):
        self.parts = 8
        self.dp = lax.axis_index("dp")
        self.x = self.dp // 2
        self.core = self.dp % 2
        self.t = lax.axis_index("tensor")

    def swap_dp(self, value, bit):
        return lax.ppermute(value, "dp", [(i, i ^ bit) for i in range(4)])

    def swap_t(self, value, bit):
        return lax.ppermute(value, "tensor", [(i, i ^ bit) for i in range(8)])

    def sum_dp(self, value):
        for bit in (1, 2):
            value = value + self.swap_dp(value, bit)
        return value

    def joined(self, mine, other, flag, axis):
        first = jnp.where(flag == 0, mine, other)
        second = jnp.where(flag == 0, other, mine)
        return jnp.concatenate([first, second], axis=axis)

    def gather(self, shard, x_first=False):
        rows, width = shard.shape
        held = shard.reshape(4, 1, rows // 4, width)
        held = lax.dynamic_index_in_dim(held, self.dp, 0, keepdims=False)
        held = held[:, None]
        for bit in (4, 2):
            held = jnp.concatenate([held, self.swap_t(held, bit)], axis=0)
        for axis in ("x", "y") if x_first else ("y", "x"):
            if axis == "y":
                held = jnp.concatenate([held, self.swap_t(held, 1)], axis=0)
            else:
                held = self.joined(held, self.swap_dp(held, 2), self.x, 1)
        held = held[:, :, None]
        held = self.joined(held, self.swap_dp(held, 1), self.core, 2)
        return held.reshape(8, rows, width)

    def gather_bias(self, shard):
        held = shard[None]
        for bit in (4, 2, 1):
            held = jnp.concatenate([held, self.swap_t(held, bit)], axis=0)
        return held

    def columns(self, array):
        quarter = array.shape[-1] // 4
        parts = [array[..., n * quarter : (n + 1) * quarter] for n in range(4)]
        chosen = []
        for k in range(2):
            pair = [jnp.where(self.core == k, parts[2 * n], parts[2 * n + 1]) for n in range(2)]
            for i in range(2):
                chosen.append(jnp.where(self.x == i, pair[0], pair[1]))
        return jnp.concatenate(chosen, axis=-1)

    def scatter(self, grads, x_first=True):
        half = grads.shape[-1] // 2
        grads = grads[..., :half] + self.swap_dp(grads[..., half:], 1)
        for axis in ("x", "y") if x_first else ("y", "x"):
            if axis == "y":
                grads = grads[:4] + self.swap_t(grads[4:], 1)
            else:
                half = grads.shape[-1] // 2
                grads = grads[..., :half] + self.swap_dp(grads[..., half:], 2)
        grads = grads[:2] + self.swap_t(grads[2:], 2)
        return grads[0].astype(jnp.float32) + self.swap_t(grads[1], 4).astype(jnp.float32)

    def scatter_bias(self, grads):
        grads = self.sum_dp(grads)
        for count, bit in ((4, 1), (2, 2), (1, 4)):
            grads = grads[:count] + self.swap_t(grads[count:], bit)
        size = grads.shape[1] // 4
        return lax.dynamic_slice_in_dim(grads[0], self.dp * size, size, 0)

    def scatter_vectors(self, vectors):
        vectors = self.sum_dp(vectors)
        for bit in (1, 2, 4):
            vectors = vectors + self.swap_t(vectors, bit)
        size = vectors.shape[1] // 32
        return lax.dynamic_slice_in_dim(vectors, (self.dp * 8 + self.t) * size, size, 1)

    def scatter_qkv(self, grads):
        kinds, width, cols = grads.shape
        grads = grads.reshape(kinds, 2, 2, width // 4, cols)
        low, high = grads[:, :, 0], grads[:, :, 1]
        mine = jnp.where(self.core == 0, low, high)
        grads = mine + self.swap_dp(jnp.where(self.core == 0, high, low), 1)
        low, high = grads[:, 0], grads[:, 1]
        mine = jnp.where(self.x == 0, low, high)
        return mine.astype(jnp.float32) + self.swap_dp(
            jnp.where(self.x == 0, high, low), 2
        ).astype(jnp.float32)

    def scatter_qv(self, grads):
        grads = self.sum_dp(grads)
        size = grads.shape[1] // 4
        return lax.dynamic_slice_in_dim(grads, self.dp * size, size, 1)

    def to_tokens(self, context):
        segment = context.shape[0] // 8
        blocks = []
        for slot in SLOTS:
            start = (self.t ^ slot) * segment
            block = lax.dynamic_slice_in_dim(context, start, segment, 0)
            blocks.append(self.swap_t(block, slot) if slot else block)
        return jnp.stack(blocks)

    def to_heads(self, blocks):
        whole = jnp.zeros((8,) + blocks.shape[1:], blocks.dtype)
        for place, slot in enumerate(SLOTS):
            block = self.swap_t(blocks[place], slot) if slot else blocks[place]
            whole = lax.dynamic_update_index_in_dim(whole, block, self.t ^ slot, 0)
        return whole.reshape((-1,) + blocks.shape[2:])


def attend(q_heads, k_heads, v_heads, scale):
    half_len = q_heads.shape[0] // 2
    pieces, logsums = [], []
    for block in range(2):
        limit = (block + 1) * half_len
        scores = (
            jnp.einsum(
                "qihd,kihd->ihqk",
                q_heads[block * half_len : limit],
                k_heads[:limit],
                preferred_element_type=jnp.float32,
            )
            * scale
        )
        highest = jnp.max(scores, axis=-1, keepdims=True)
        logsum = highest + jnp.log(jnp.sum(jnp.exp(scores - highest), axis=-1, keepdims=True))
        probs_low = jnp.exp(scores - logsum).astype(jnp.bfloat16)
        pieces.append(
            jnp.einsum(
                "ihqk,kihd->qihd", probs_low, v_heads[:limit], preferred_element_type=jnp.float32
            )
        )
        logsums.append(logsum)
    return jnp.concatenate(pieces, axis=0).astype(jnp.bfloat16), logsums


def attend_back(q_heads, k_heads, v_heads, grad_ctx_heads, logsums, scale):
    seq_len = q_heads.shape[0]
    half_len = seq_len // 2
    query_grads = []
    key_total = jnp.zeros(q_heads.shape, jnp.float32)
    value_total = jnp.zeros(q_heads.shape, jnp.float32)
    for block in range(2):
        limit = (block + 1) * half_len
        rows_q = q_heads[block * half_len : limit]
        rows_grad = grad_ctx_heads[block * half_len : limit]
        scores = (
            jnp.einsum(
                "qihd,kihd->ihqk", rows_q, k_heads[:limit], preferred_element_type=jnp.float32
            )
            * scale
        )
        probs = jnp.exp(scores - logsums[block])
        probs_low = probs.astype(jnp.bfloat16)
        grad_probs = jnp.einsum(
            "qihd,kihd->ihqk", rows_grad, v_heads[:limit], preferred_element_type=jnp.float32
        )
        value_part = jnp.einsum(
            "ihqk,qihd->kihd", probs_low, rows_grad, preferred_element_type=jnp.float32
        )
        grad_scores = (
            probs * (grad_probs - jnp.sum(probs * grad_probs, axis=-1, keepdims=True))
        ).astype(jnp.bfloat16)
        query_grads.append(
            jnp.einsum(
                "ihqk,kihd->qihd", grad_scores, k_heads[:limit], preferred_element_type=jnp.float32
            )
            * scale
        )
        key_part = (
            jnp.einsum("ihqk,qihd->kihd", grad_scores, rows_q, preferred_element_type=jnp.float32)
            * scale
        )
        padding = ((0, seq_len - limit), (0, 0), (0, 0), (0, 0))
        key_total = key_total + jnp.pad(key_part, padding)
        value_total = value_total + jnp.pad(value_part, padding)
    return (
        jnp.concatenate(query_grads, axis=0).astype(jnp.bfloat16),
        key_total.astype(jnp.bfloat16),
        value_total.astype(jnp.bfloat16),
    )


def mm(left, right, dims):
    return lax.dot_general(left, right, (dims, ((), ())), preferred_element_type=jnp.float32)


def body(
    tokens,
    cotangent,
    timesteps,
    bucket,
    counts,
    qkv_weight,
    qv_bias,
    out_weight,
    out_bias,
    norm1_gain,
    norm1_bias,
    up_weight,
    up_bias,
    down_weight,
    down_bias,
    norm2_gain,
    norm2_bias,
):
    micro, segment, items_loc, width = tokens.shape
    parts = lax.axis_size("tensor")
    replicas = lax.axis_size("dp")
    move = Cube() if (replicas, parts) == (4, 8) else Plain()
    seq_len = segment * parts
    half_len = seq_len // 2
    columns = qkv_weight.shape[2]
    heads_loc = columns // HD
    scale = float(HD) ** (-0.5)
    low = jnp.bfloat16
    position = lax.axis_index("tensor") * segment + jnp.arange(segment)
    late = position >= half_len

    hiddens, gathered = [], []
    for index in range(micro):
        embedded = sinusoid(timesteps[index], width)
        temb = jnp.where(late[:, None, None], embedded[None, :, 1], embedded[None, :, 0])
        hidden = tokens[index].astype(jnp.float32) + temb
        hiddens.append(hidden)
        gathered.append(lax.all_gather(hidden.astype(low), "tensor", axis=0, tiled=True))
    out_all = move.gather(out_weight)
    up_all = move.gather(up_weight.T)
    down_all = move.gather(down_weight, x_first=True)
    bias_all = move.gather_bias(up_bias).reshape(1, -1)
    out_all = out_all.reshape(-1, width)
    up_all = up_all.reshape(-1, width)
    down_all = down_all.reshape(-1, width)
    hidden_units = up_all.shape[0]

    kept, context_rows = [], []
    for index in range(micro):
        projected = jnp.einsum(
            "sid,kdc->ksic", gathered[index], qkv_weight, preferred_element_type=jnp.float32
        )
        shape = (seq_len, items_loc, heads_loc, HD)
        q_heads = (projected[0] + qv_bias[0]).astype(low).reshape(shape)
        k_heads = projected[1].astype(low).reshape(shape)
        v_heads = (projected[2] + qv_bias[1]).astype(low).reshape(shape)
        context, logsums = attend(q_heads, k_heads, v_heads, scale)
        kept.append((q_heads, k_heads, v_heads, logsums))
        blocks = move.to_tokens(context.reshape(seq_len, items_loc, columns))
        context_rows.append(
            blocks.transpose(1, 2, 0, 3).reshape(segment * items_loc, parts * columns)
        )
    context_rows = jnp.concatenate(context_rows, axis=0)

    rows = micro * segment * items_loc
    hidden = jnp.stack(hiddens).reshape(rows, width)
    attention = mm(context_rows, out_all, ((1,), (0,)))
    normed, unit_one, inverse_one = norm_forward(
        hidden + (attention + out_bias), norm1_gain, norm1_bias
    )
    normed_low = normed.astype(low)
    pre = mm(normed_low, up_all, ((1,), (1,))) + bias_all
    gate = 0.5 * (1.0 + lax.erf(pre * INV_ROOT_TWO))
    act_low = (pre * gate).astype(low)
    slope = gate + pre * jnp.exp(-0.5 * pre * pre) * INV_ROOT_TWO_PI
    branch = mm(act_low, down_all, ((1,), (0,)))
    result, unit_two, inverse_two = norm_forward(
        normed + (branch + down_bias), norm2_gain, norm2_bias
    )
    layer_out = result.astype(low).reshape(tokens.shape)

    count_f = counts.astype(jnp.float32)
    total = move.sum_dp(jnp.sum(count_f))
    item_weight = count_f * float(micro * items_loc * replicas) / total
    keep = jnp.where(late[None, :, None], bucket[:, None, :], 1).astype(jnp.float32)
    factor = (keep * item_weight[:, None, :]).reshape(rows, 1)
    grad_out = cotangent.astype(jnp.float32).reshape(rows, width) * factor
    gain_two_grad = jnp.sum(grad_out * unit_two, axis=0)
    shift_two_grad = jnp.sum(grad_out, axis=0)
    grad_sum = norm_backward(grad_out, unit_two, inverse_two, norm2_gain)
    down_bias_grad = jnp.sum(grad_sum, axis=0)
    grad_sum_low = grad_sum.astype(low)

    down_grad = mm(act_low, move.columns(grad_sum_low), ((0,), (0,))).astype(low)
    down_grad = move.scatter(down_grad.reshape(parts, -1, width), x_first=True)
    grad_act = mm(grad_sum_low, down_all, ((1,), (1,)))
    grad_pre = (grad_act * slope).astype(low)
    up_bias_grad = move.scatter_bias(
        jnp.sum(grad_pre, axis=0, dtype=jnp.float32).reshape(parts, -1)
    )
    up_grad = mm(grad_pre, move.columns(normed_low), ((0,), (0,))).astype(low)
    up_grad = move.scatter(up_grad.reshape(parts, -1, width), x_first=False)
    grad_normed = grad_sum + mm(grad_pre, up_all, ((1,), (0,)))
    gain_one_grad = jnp.sum(grad_normed * unit_one, axis=0)
    shift_one_grad = jnp.sum(grad_normed, axis=0)
    grad_mixed = norm_backward(grad_normed, unit_one, inverse_one, norm1_gain)
    out_bias_grad = jnp.sum(grad_mixed, axis=0)
    grad_mixed_low = grad_mixed.astype(low)
    vector_grads = move.scatter_vectors(
        jnp.stack(
            [
                out_bias_grad,
                gain_one_grad,
                shift_one_grad,
                down_bias_grad,
                gain_two_grad,
                shift_two_grad,
            ]
        )
    )
    out_grad = mm(context_rows, move.columns(grad_mixed_low), ((0,), (0,))).astype(low)
    out_grad = move.scatter(out_grad.reshape(parts, -1, width), x_first=True)
    grad_context = mm(grad_mixed_low, out_all, ((1,), (1,))).astype(low)
    grad_context = grad_context.reshape(micro, segment, items_loc, parts, columns)

    qkv_total, bias_total, input_grads = None, None, []
    for index in range(micro):
        q_heads, k_heads, v_heads, logsums = kept[index]
        grad_heads = move.to_heads(grad_context[index].transpose(2, 0, 1, 3))
        grads = attend_back(
            q_heads, k_heads, v_heads, grad_heads.reshape(q_heads.shape), logsums, scale
        )
        grad_stack = jnp.stack(
            [part.reshape(seq_len, items_loc, columns) for part in grads]
        )
        bias_grad = jnp.stack(
            [
                jnp.sum(grad_stack[0], axis=(0, 1), dtype=jnp.float32),
                jnp.sum(grad_stack[2], axis=(0, 1), dtype=jnp.float32),
            ]
        )
        input_grads.append(
            lax.psum_scatter(
                jnp.einsum(
                    "ksic,kdc->sid", grad_stack, qkv_weight, preferred_element_type=jnp.float32
                ).astype(low),
                "tensor",
                scatter_dimension=0,
                tiled=True,
            )
        )
        qkv_part = jnp.einsum(
            "sid,ksic->kdc", gathered[index], grad_stack, preferred_element_type=jnp.float32
        )
        qkv_total = qkv_part if qkv_total is None else qkv_total + qkv_part
        bias_total = bias_grad if bias_total is None else bias_total + bias_grad
    qkv_grad = move.scatter_qkv(qkv_total.astype(low))
    qv_bias_grad = move.scatter_qv(bias_total)
    tokens_grad = grad_mixed.reshape(tokens.shape) + jnp.stack(input_grads).astype(jnp.float32)
    return (
        layer_out,
        tokens_grad,
        qkv_grad.astype(jnp.float32),
        qv_bias_grad,
        out_grad.astype(jnp.float32),
        up_grad.astype(jnp.float32).T,
        up_bias_grad,
        down_grad.astype(jnp.float32),
        vector_grads,
    )


def solution(mesh):
    placed = (
        P(None, "tensor", "dp", None),
        P(None, "tensor", "dp", None),
        P(None, "dp", None),
        P(None, "dp"),
        P(None, "dp"),
        P(None, None, "tensor"),
        P(None, "tensor"),
        P("tensor", None),
        P(),
        P(),
        P(),
        P(None, "tensor"),
        P("tensor"),
        P("tensor", None),
        P(),
        P(),
        P(),
    )
    return jax.shard_map(
        body,
        mesh=mesh,
        in_specs=placed,
        out_specs=(
            P(None, "tensor", "dp", None),
            P(None, "tensor", "dp", None),
            P(None, "dp", "tensor"),
            P(None, ("tensor", "dp")),
            P("tensor", "dp"),
            P("dp", "tensor"),
            P(("tensor", "dp")),
            P("tensor", "dp"),
            P(None, ("dp", "tensor")),
        ),
        check_vma=False,
    )
```

```python
import functools
import math

import jax
import jax.numpy as jnp
from jax import lax
from jax.experimental import pallas as pl
from jax.experimental.pallas import tpu as pltpu
from jax.sharding import PartitionSpec as P

HD = 64


EPS = 1e-05
INV_ROOT_TWO = 1.0 / math.sqrt(2.0)
INV_ROOT_TWO_PI = 1.0 / math.sqrt(2.0 * math.pi)

SLOTS = (0, 4, 2, 6, 1, 5, 3, 7)


def sinusoid(steps, width):
    half_width = width // 2
    freqs = jnp.exp(jnp.arange(half_width).astype(jnp.float32) * (-2.0 * math.log(10000.0) / width))
    angles = steps.astype(jnp.float32)[..., None] * freqs
    return jnp.concatenate([jnp.sin(angles), jnp.cos(angles)], axis=-1)


def norm_forward(values, gain, shift):
    average = jnp.mean(values, axis=-1, keepdims=True)
    centred = values - average
    spread = jnp.mean(centred * centred, axis=-1, keepdims=True)
    inverse = lax.rsqrt(spread + EPS)
    unit = centred * inverse
    return (unit * gain + shift, unit, inverse)


def norm_backward(grad, unit, inverse, gain):
    scaled = grad * gain
    first = jnp.mean(scaled, axis=-1, keepdims=True)
    second = jnp.mean(scaled * unit, axis=-1, keepdims=True)
    return inverse * (scaled - first - unit * second)


MESH_ID = pl.DeviceIdType.MESH
ANY = pl.BlockSpec(memory_space=pl.ANY)
VMEM = pl.BlockSpec(memory_space=pltpu.VMEM)


def flipped(t, slot):
    bits = [t % 2, (t // 2) % 2, t // 4]
    return sum(
        ((1 - bit) if (slot >> place) & 1 else bit) * (1 << place)
        for place, bit in enumerate(bits)
    )


def remote(source, target, send, receive, device):
    return pltpu.make_async_remote_copy(
        src_ref=source,
        dst_ref=target,
        send_sem=send,
        recv_sem=receive,
        device_id={"tensor": device},
        device_id_type=MESH_ID,
    )


def gather_kernel(x_ref, o_ref, own_sem, up_s, up_r, down_s, down_r, side_s, side_r):
    t = lax.axis_index("tensor")
    z, y = t // 2, t % 2
    across = z * 2 + 1 - y
    has_up = jnp.where(z < 3, 1, 0)
    has_down = jnp.where(z > 0, 1, 0)
    barrier = pltpu.get_barrier_semaphore()
    pl.semaphore_signal(barrier, inc=1, device_id={"tensor": across}, device_id_type=MESH_ID)

    @pl.when(z < 3)
    def _():
        pl.semaphore_signal(barrier, inc=1, device_id={"tensor": t + 2}, device_id_type=MESH_ID)

    @pl.when(z > 0)
    def _():
        pl.semaphore_signal(barrier, inc=1, device_id={"tensor": t - 2}, device_id_type=MESH_ID)

    pl.semaphore_wait(barrier, 1 + has_up + has_down)

    def sideways(source, k):
        return remote(source, o_ref.at[k * 2 + y], side_s.at[k], side_r.at[k], across)

    def upwards(source, k):
        return remote(source, o_ref.at[k * 2 + y], up_s.at[k], up_r.at[k], t + 2)

    def downwards(source, k):
        return remote(source, o_ref.at[k * 2 + y], down_s.at[k], down_r.at[k], t - 2)

    @pl.when(z < 3)
    def _():
        upwards(x_ref, z).start()

    @pl.when(z > 0)
    def _():
        downwards(x_ref, z).start()

    sideways(x_ref, z).start()
    own = pltpu.make_async_copy(x_ref, o_ref.at[t], own_sem)
    own.start()
    for step in range(1, 4):

        @pl.when(z - step >= 0)
        def _():
            k = z - step
            block = o_ref.at[k * 2 + y]
            upwards(block, k).wait_recv()

            @pl.when(z < 3)
            def _():
                upwards(block, k).start()

            sideways(block, k).start()

        @pl.when(z + step <= 3)
        def _():
            k = z + step
            block = o_ref.at[k * 2 + y]
            downwards(block, k).wait_recv()

            @pl.when(z > 0)
            def _():
                downwards(block, k).start()

            sideways(block, k).start()

    for k in range(4):
        remote(x_ref, o_ref.at[k * 2 + 1 - y], side_s.at[k], side_r.at[k], across).wait_recv()
        sideways(x_ref, k).wait_send()

        @pl.when((z < 3) & (k <= z))
        def _():
            upwards(x_ref, k).wait_send()

        @pl.when((z > 0) & (k >= z))
        def _():
            downwards(x_ref, k).wait_send()

    own.wait()


def gather_tokens(chunk):
    size = chunk.size * 2
    return pl.pallas_call(
        gather_kernel,
        out_shape=jax.ShapeDtypeStruct((8,) + chunk.shape, chunk.dtype),
        in_specs=[VMEM],
        out_specs=ANY,
        scratch_shapes=[pltpu.SemaphoreType.DMA] + [pltpu.SemaphoreType.DMA((4,))] * 6,
        compiler_params=pltpu.CompilerParams(collective_id=1, has_side_effects=True),
        cost_estimate=pl.CostEstimate(flops=0, bytes_accessed=80 * size, transcendentals=0),
        name="gather_tokens",
    )(chunk)


def greet_all(t):
    barrier = pltpu.get_barrier_semaphore()
    for slot in range(1, 8):
        pl.semaphore_signal(
            barrier, inc=1, device_id={"tensor": flipped(t, slot)}, device_id_type=MESH_ID
        )
    pl.semaphore_wait(barrier, 7)


def tokens_kernel(first_ref, second_ref, o_ref, own_sems, send_sems, recv_sems):
    t = lax.axis_index("tensor")
    segment, cols = first_ref.shape[1] // 8, first_ref.shape[2]
    greet_all(t)
    copies = []
    for index, ref in enumerate((first_ref, second_ref)):
        rows = pl.ds(index * segment, segment)
        for place, slot in enumerate(SLOTS):
            peer = flipped(t, slot)
            start = pl.multiple_of(peer * segment, segment)
            source = ref.at[0, pl.ds(start, segment), :]
            target = o_ref.at[rows, pl.ds(place * cols, cols)]
            if slot:
                copy = remote(
                    source, target, send_sems.at[index, place], recv_sems.at[index, place], peer
                )
            else:
                copy = pltpu.make_async_copy(source, target, own_sems.at[index])
            copy.start()
            copies.append(copy)
    for copy in copies:
        copy.wait()


def tokens_of_heads(first, second):
    _, seq, cols = first.shape
    return pl.pallas_call(
        tokens_kernel,
        out_shape=jax.ShapeDtypeStruct((seq // 4, 8 * cols), first.dtype),
        in_specs=[VMEM, VMEM],
        out_specs=ANY,
        scratch_shapes=[
            pltpu.SemaphoreType.DMA((2,)),
            pltpu.SemaphoreType.DMA((2, 8)),
            pltpu.SemaphoreType.DMA((2, 8)),
        ],
        compiler_params=pltpu.CompilerParams(collective_id=2, has_side_effects=True),
        cost_estimate=pl.CostEstimate(flops=0, bytes_accessed=80 << 20, transcendentals=0),
        name="tokens_of_heads",
    )(first, second)


def heads_kernel(x_ref, first_ref, second_ref, own_sems, send_sems, recv_sems):
    t = lax.axis_index("tensor")
    segment, cols = first_ref.shape[1] // 8, first_ref.shape[2]
    greet_all(t)
    copies = []
    mine = pl.ds(pl.multiple_of(t * segment, segment), segment)
    for index, ref in enumerate((first_ref, second_ref)):
        rows = pl.ds(index * segment, segment)
        for place, slot in enumerate(SLOTS):
            source = x_ref.at[rows, pl.ds(place * cols, cols)]
            if slot:
                peer = flipped(t, slot)
                start = pl.ds(pl.multiple_of(t * segment, segment), segment)
                copy = remote(
                    source,
                    ref.at[0, start, :],
                    send_sems.at[index, place],
                    recv_sems.at[index, place],
                    peer,
                )
            else:
                copy = pltpu.make_async_copy(source, ref.at[0, mine, :], own_sems.at[index])
            copy.start()
            copies.append((copy, ref, index, place, slot))
    for copy, ref, index, place, slot in copies:
        if slot:
            copy.wait_send()
            peer = flipped(t, slot)
            start = pl.ds(pl.multiple_of(peer * segment, segment), segment)
            remote(
                x_ref.at[pl.ds(index * segment, segment), pl.ds(place * cols, cols)],
                ref.at[0, start, :],
                send_sems.at[index, place],
                recv_sems.at[index, place],
                peer,
            ).wait_recv()
        else:
            copy.wait()


def heads_of_tokens(array):
    rows, width = array.shape
    shape = jax.ShapeDtypeStruct((1, rows * 4, width // 8), array.dtype)
    return pl.pallas_call(
        heads_kernel,
        out_shape=[shape, shape],
        in_specs=[VMEM],
        out_specs=[ANY, ANY],
        scratch_shapes=[
            pltpu.SemaphoreType.DMA((2,)),
            pltpu.SemaphoreType.DMA((2, 8)),
            pltpu.SemaphoreType.DMA((2, 8)),
        ],
        compiler_params=pltpu.CompilerParams(collective_id=3, has_side_effects=True),
        cost_estimate=pl.CostEstimate(flops=0, bytes_accessed=80 << 20, transcendentals=0),
        name="heads_of_tokens",
    )(array)

def scatter_kernel(
    x_ref, o_ref, side_buf, up_buf, down_buf, sent_buf, side_s, side_r, up_s, up_r, down_s, down_r
):
    t = lax.axis_index("tensor")
    z, y = t // 2, t % 2
    across = z * 2 + 1 - y
    lower = z < 2
    order = [
        jnp.where(lower, 3, 0),
        jnp.where(lower, 2, 1),
        jnp.where(lower, 1 - z, 5 - z),
        z,
    ]
    barrier = pltpu.get_barrier_semaphore()
    pl.semaphore_signal(barrier, inc=1, device_id={"tensor": across}, device_id_type=MESH_ID)

    @pl.when(z < 3)
    def _():
        pl.semaphore_signal(barrier, inc=1, device_id={"tensor": t + 2}, device_id_type=MESH_ID)

    @pl.when(z > 0)
    def _():
        pl.semaphore_signal(barrier, inc=1, device_id={"tensor": t - 2}, device_id_type=MESH_ID)

    pl.semaphore_wait(barrier, 1 + jnp.where(z < 3, 1, 0) + jnp.where(z > 0, 1, 0))

    def sideways(k):
        return remote(
            x_ref.at[k * 2 + 1 - y], side_buf.at[k], side_s.at[k], side_r.at[k], across
        )

    def upwards(k):
        return remote(sent_buf.at[k], up_buf.at[k], up_s.at[k], up_r.at[k], t + 2)

    def downwards(k):
        return remote(sent_buf.at[k], down_buf.at[k], down_s.at[k], down_r.at[k], t - 2)

    for k in order:
        sideways(k).start()
    for k in order[:3]:
        sideways(k).wait_recv()
        total = x_ref[k * 2 + y].astype(jnp.float32) + side_buf[k].astype(jnp.float32)

        @pl.when((k > z) & (z == 0))
        def _():
            sent_buf[k] = total.astype(sent_buf.dtype)
            upwards(k).start()

        @pl.when((k > z) & (z > 0))
        def _():
            upwards(k).wait_recv()
            sent_buf[k] = (total + up_buf[k].astype(jnp.float32)).astype(sent_buf.dtype)
            upwards(k).start()

        @pl.when((k < z) & (z == 3))
        def _():
            sent_buf[k] = total.astype(sent_buf.dtype)
            downwards(k).start()

        @pl.when((k < z) & (z < 3))
        def _():
            downwards(k).wait_recv()
            sent_buf[k] = (total + down_buf[k].astype(jnp.float32)).astype(sent_buf.dtype)
            downwards(k).start()

    sideways(z).wait_recv()
    o_ref[...] = x_ref[z * 2 + y].astype(jnp.float32) + side_buf[z].astype(jnp.float32)

    @pl.when(z > 0)
    def _():
        upwards(z).wait_recv()
        o_ref[...] += up_buf[z].astype(jnp.float32)

    @pl.when(z < 3)
    def _():
        downwards(z).wait_recv()
        o_ref[...] += down_buf[z].astype(jnp.float32)

    for k in range(4):
        sideways(k).wait_send()

        @pl.when(k > z)
        def _():
            upwards(k).wait_send()

        @pl.when(k < z)
        def _():
            downwards(k).wait_send()


def scatter_tokens(partial):
    chunk = partial.shape[1:]
    block = pltpu.VMEM((4,) + chunk, partial.dtype)
    return pl.pallas_call(
        scatter_kernel,
        out_shape=jax.ShapeDtypeStruct(chunk, jnp.float32),
        in_specs=[VMEM],
        out_specs=VMEM,
        scratch_shapes=[block] * 4 + [pltpu.SemaphoreType.DMA((4,))] * 6,
        compiler_params=pltpu.CompilerParams(
            collective_id=4, has_side_effects=True, vmem_limit_bytes=40 << 20
        ),
        cost_estimate=pl.CostEstimate(flops=0, bytes_accessed=160 << 20, transcendentals=0),
        name="scatter_tokens",
    )(partial)


def head_masks(heads, columns, scale):
    lane = lax.broadcasted_iota(jnp.int32, (1, columns), 1) // HD
    return [jnp.where(lane == head, scale, 0.0).astype(jnp.float32) for head in range(heads)]


def by_head(tile, masks):
    wide = tile.astype(jnp.float32)
    return jnp.concatenate([wide * mask for mask in masks], axis=0).astype(tile.dtype)


def join_heads(sums, heads, tile):
    parts = [
        sums[head * HD : (head + 1) * HD, head * tile : (head + 1) * tile] for head in range(heads)
    ]
    return (jnp.concatenate(parts, axis=0) if heads > 1 else parts[0]).T


def turned(left, right):
    return lax.dot_general(
        left, right, (((1,), (1,)), ((), ())), preferred_element_type=jnp.float32
    )


def plain(left, right):
    return lax.dot_general(
        left, right, (((1,), (0,)), ((), ())), preferred_element_type=jnp.float32
    )


def forward_kernel(heads, half_steps, q_ref, k_ref, v_ref, out_ref, lse_ref, vt_ref):
    step = pl.program_id(1)
    tile, columns = q_ref.shape[2], q_ref.shape[3]
    seq = k_ref.shape[2]

    @pl.when(step == 0)
    def _():
        vt_ref[...] = v_ref[0, 0].astype(jnp.float32).T.astype(jnp.bfloat16)

    def tokens(limit):
        masks = head_masks(heads, columns, HD**-0.5)
        queries = by_head(q_ref[0, 0], masks)
        scores = turned(k_ref[0, 0, :limit, :], queries)
        highest = jnp.max(scores, axis=0, keepdims=True)
        probs = jnp.exp(scores - highest)
        total = jnp.sum(probs, axis=0, keepdims=True)
        sums = plain(vt_ref[:, :limit], probs.astype(jnp.bfloat16)) * (1.0 / total)
        out_ref[0] = join_heads(sums, heads, tile).astype(out_ref.dtype)
        logsum = highest + jnp.log(total)
        for head in range(heads):
            lse_ref[0, head : head + 1, :] = logsum[:, head * tile : (head + 1) * tile]

    @pl.when(step < half_steps)
    def _():
        tokens(seq // 2)

    @pl.when(step >= half_steps)
    def _():
        tokens(seq)


def attend(qkv, tile):
    _, items, seq, columns = qkv.shape
    heads = columns // HD
    steps = seq // tile
    pairs = seq * seq * 3 // 4 * items * heads
    return pl.pallas_call(
        functools.partial(forward_kernel, heads, steps // 2),
        grid=(items, steps),
        in_specs=[
            pl.BlockSpec((1, 1, tile, columns), lambda i, j: (0, i, j, 0)),
            pl.BlockSpec((1, 1, seq, columns), lambda i, j: (1, i, 0, 0)),
            pl.BlockSpec((1, 1, seq, columns), lambda i, j: (2, i, 0, 0)),
        ],
        out_specs=[
            pl.BlockSpec((1, tile, columns), lambda i, j: (i, j, 0)),
            pl.BlockSpec((1, heads, tile), lambda i, j: (i, 0, j)),
        ],
        out_shape=[
            jax.ShapeDtypeStruct((items, seq, columns), jnp.bfloat16),
            jax.ShapeDtypeStruct((items, heads, seq), jnp.float32),
        ],
        scratch_shapes=[pltpu.VMEM((columns, seq), jnp.bfloat16)],
        cost_estimate=pl.CostEstimate(
            flops=pairs * HD * 16, transcendentals=pairs, bytes_accessed=qkv.size * 3
        ),
        name="attend",
    )(qkv, qkv, qkv)


def backward_kernel(
    heads, half_steps, q_ref, k_ref, v_ref, out_ref, lse_ref, grad_ref, all_ref, kt_ref, dk_ref, dv_ref
):
    step = pl.program_id(1)
    tile, columns = q_ref.shape[2], q_ref.shape[3]
    seq = k_ref.shape[2]
    scale = HD**-0.5

    @pl.when(step == 0)
    def _():
        kt_ref[...] = k_ref[0, 0].astype(jnp.float32).T.astype(jnp.bfloat16)
        dk_ref[...] = jnp.zeros_like(dk_ref)
        dv_ref[...] = jnp.zeros_like(dv_ref)

    def tokens(limit):
        queries = by_head(q_ref[0, 0], head_masks(heads, columns, scale))
        ones = head_masks(heads, columns, 1.0)
        grads = by_head(grad_ref[0], ones)
        product = grad_ref[0].astype(jnp.float32) * out_ref[0].astype(jnp.float32)
        rows = lax.broadcasted_iota(jnp.int32, (8, columns), 0)
        lanes = lax.broadcasted_iota(jnp.int32, (8, columns), 1) // HD
        picks = jnp.where(rows == lanes, 1.0, 0.0)
        delta_rows = lax.dot_general(
            picks,
            product,
            (((1,), (1,)), ((), ())),
            precision=lax.Precision.HIGHEST,
            preferred_element_type=jnp.float32,
        )
        delta = jnp.concatenate([delta_rows[h : h + 1] for h in range(heads)], axis=1)
        logsum = jnp.concatenate([lse_ref[0, h : h + 1, :] for h in range(heads)], axis=1)
        scores = turned(k_ref[0, 0, :limit, :], queries)
        probs = jnp.exp(scores - logsum)
        dv_ref[:limit, :] += plain(probs.astype(jnp.bfloat16), grads)
        grad_probs = turned(v_ref[0, 0, :limit, :], grads)
        grad_scores = (probs * (grad_probs - delta)).astype(jnp.bfloat16)
        dk_ref[:limit, :] += plain(grad_scores, queries)
        sums = plain(kt_ref[:, :limit], grad_scores) * scale
        start = pl.multiple_of(step * tile, tile)
        all_ref[0, 0, pl.ds(start, tile), :] = join_heads(sums, heads, tile).astype(all_ref.dtype)

    @pl.when(step < half_steps)
    def _():
        tokens(seq // 2)

    @pl.when(step >= half_steps)
    def _():
        tokens(seq)

    @pl.when(step == pl.num_programs(1) - 1)
    def _():
        all_ref[1, 0] = dk_ref[...].astype(all_ref.dtype)
        all_ref[2, 0] = dv_ref[...].astype(all_ref.dtype)


def attend_back(qkv, context, logsum, grad_context, tile):
    _, items, seq, columns = qkv.shape
    heads = columns // HD
    steps = seq // tile
    pairs = seq * seq * 3 // 4 * items * heads
    return pl.pallas_call(
        functools.partial(backward_kernel, heads, steps // 2),
        grid=(items, steps),
        in_specs=[
            pl.BlockSpec((1, 1, tile, columns), lambda i, j: (0, i, j, 0)),
            pl.BlockSpec((1, 1, seq, columns), lambda i, j: (1, i, 0, 0)),
            pl.BlockSpec((1, 1, seq, columns), lambda i, j: (2, i, 0, 0)),
            pl.BlockSpec((1, tile, columns), lambda i, j: (i, j, 0)),
            pl.BlockSpec((1, heads, tile), lambda i, j: (i, 0, j)),
            pl.BlockSpec((1, tile, columns), lambda i, j: (i, j, 0)),
        ],
        out_specs=pl.BlockSpec((3, 1, seq, columns), lambda i, j: (0, i, 0, 0)),
        out_shape=jax.ShapeDtypeStruct((3, items, seq, columns), jnp.bfloat16),
        scratch_shapes=[
            pltpu.VMEM((columns, seq), jnp.bfloat16),
            pltpu.VMEM((seq, columns), jnp.float32),
            pltpu.VMEM((seq, columns), jnp.float32),
        ],
        cost_estimate=pl.CostEstimate(
            flops=pairs * HD * 40, transcendentals=pairs, bytes_accessed=qkv.size * 5
        ),
        name="attend_back",
    )(qkv, qkv, qkv, context, logsum, grad_context)


def mm(left, right, dims):
    return lax.dot_general(left, right, (dims, ((), ())), preferred_element_type=jnp.float32)


def swap_dp(value, bit):
    return lax.ppermute(value, "dp", [(i, i ^ bit) for i in range(4)])


def swap_t(value, bit):
    return lax.ppermute(value, "tensor", [(i, i ^ bit) for i in range(8)])


def gate(flows, *arrays):
    held, arrays = lax.optimization_barrier((tuple(flow.value for flow in flows), arrays))
    for flow, value in zip(flows, held):
        flow.value = value
    return arrays[0] if len(arrays) == 1 else arrays


class Whole:
    def __init__(self, shard, x_first):
        self.value = lax.all_gather(shard, "tensor", axis=0, tiled=False)

    def step(self):
        pass

    def matrix(self):
        return self.value.reshape(-1, self.value.shape[-1])


class WholeGrad:
    def __init__(self, left, right, x_first):
        self.value = mm(left, right, ((0,), (0,))).astype(jnp.bfloat16)

    def join(self):
        pass

    def step(self):
        pass

    def shard(self):
        grads = self.value.reshape(lax.axis_size("tensor"), -1, self.value.shape[-1])
        part = lax.psum_scatter(grads, "tensor", scatter_dimension=0, tiled=True)[0]
        return lax.psum_scatter(part, "dp", scatter_dimension=1, tiled=True)


def joined(mine, other, flag, axis):
    first = jnp.where(flag == 0, mine, other)
    second = jnp.where(flag == 0, other, mine)
    return jnp.concatenate([first, second], axis=axis)


class Cube:
    def __init__(self, shard, x_first):
        rows, width = shard.shape
        self.rows = rows
        self.path = ["z2", "z1"] + (["x", "y"] if x_first else ["y", "x"]) + ["core"]
        quarters = shard.reshape(4, 1, 1, 1, rows // 4, width)
        self.value = lax.dynamic_index_in_dim(quarters, lax.axis_index("dp"), 0, keepdims=False)

    def step(self):
        held, axis = self.value, self.path.pop(0)
        dp = lax.axis_index("dp")
        if axis == "x":
            self.value = joined(held, swap_dp(held, 2), dp // 2, 1)
        elif axis == "core":
            self.value = joined(held, swap_dp(held, 1), dp % 2, 2)
        else:
            other = swap_t(held, {"z2": 4, "z1": 2, "y": 1}[axis])
            self.value = jnp.concatenate([held, other], axis=0)

    def matrix(self):
        return self.value.reshape(-1, self.value.shape[-1])


class CubeGrad:
    def __init__(self, left, right, x_first):
        self.left, self.keep = left, right[0]
        self.path = (["x", "y"] if x_first else ["y", "x"]) + ["z1", "z2"]
        self.sent = mm(left, right[1], ((0,), (0,))).astype(jnp.bfloat16)
        self.other = swap_dp(self.sent, 1)

    def join(self):
        total = mm(self.left, self.keep, ((0,), (0,))) + self.other.astype(jnp.float32)
        self.value = total.astype(jnp.bfloat16).reshape(8, -1, total.shape[-1])

    def step(self):
        grads, axis = self.value, self.path.pop(0)
        if axis == "x":
            half = grads.shape[-1] // 2
            self.value = grads[..., :half] + swap_dp(grads[..., half:], 2)
        else:
            half = grads.shape[0] // 2
            other = swap_t(grads[half:], {"z2": 4, "z1": 2, "y": 1}[axis])
            self.value = grads[:half] + other

    def shard(self):
        return self.value[0]


def cube_columns(array):
    dp = lax.axis_index("dp")
    x, core = dp // 2, dp % 2
    quarter = array.shape[-1] // 4
    parts = [array[..., n * quarter : (n + 1) * quarter] for n in range(4)]
    chosen = []
    for k in range(2):
        pair = [jnp.where(core == k, parts[2 * n], parts[2 * n + 1]) for n in range(2)]
        halves = [jnp.where(x == i, pair[0], pair[1]) for i in range(2)]
        chosen.append(jnp.concatenate(halves, axis=-1))
    return chosen


def scatter_qkv(grads):
    dp = lax.axis_index("dp")
    x, core = dp // 2, dp % 2
    kinds, width, cols = grads.shape
    grads = grads.reshape(kinds, 2, 2, width // 4, cols)
    early, later = grads[:, :, 0], grads[:, :, 1]
    grads = jnp.where(core == 0, early, later) + swap_dp(jnp.where(core == 0, later, early), 1)
    early, later = grads[:, 0], grads[:, 1]
    mine = jnp.where(x == 0, early, later).astype(jnp.float32)
    return mine + swap_dp(jnp.where(x == 0, later, early), 2).astype(jnp.float32)


def sum_small(vectors, bias):
    dp, t = lax.axis_index("dp"), lax.axis_index("tensor")
    rows = bias.reshape(8, -1, 128)
    packed = jnp.concatenate([vectors.reshape(-1, 128), bias.reshape(-1, 128)], axis=0)
    count = packed.shape[0] - rows.shape[0] * rows.shape[1]
    for bit in (1, 2):
        packed = packed + swap_dp(packed, bit)
    for bit in (1, 2, 4):
        other = swap_t(packed, bit)
        slots = other[count:].reshape(rows.shape)
        order = [SLOTS.index(slot ^ bit) for slot in SLOTS]
        slots = jnp.concatenate([slots[n : n + 1] for n in order], axis=0)
        packed = packed + jnp.concatenate([other[:count], slots.reshape(-1, 128)], axis=0)
    summed = packed[:count].reshape(vectors.shape)
    size = vectors.shape[1] // 32
    summed = lax.dynamic_slice_in_dim(summed, (dp * 8 + t) * size, size, 1)
    own = packed[count : count + rows.shape[1]].reshape(-1)
    size = own.shape[0] // 4
    return summed, lax.dynamic_slice_in_dim(own, dp * size, size, 0)


def body(
    tokens,
    cotangent,
    timesteps,
    bucket,
    counts,
    qkv_weight,
    qv_bias,
    out_weight,
    out_bias,
    norm1_gain,
    norm1_bias,
    up_weight,
    up_bias,
    down_weight,
    down_bias,
    norm2_gain,
    norm2_bias,
):
    micro, segment, items_loc, width = tokens.shape
    parts = lax.axis_size("tensor")
    replicas = lax.axis_size("dp")
    seq_len = segment * parts
    half_len = seq_len // 2
    columns = qkv_weight.shape[2]
    low = jnp.bfloat16
    cube = (replicas, parts, micro, items_loc) == (4, 8, 2, 1) and columns % 128 == 0
    weight, weight_grad = (Cube, CubeGrad) if cube else (Whole, WholeGrad)
    pick = cube_columns if cube else (lambda array: array)
    tile = min(512, half_len)
    position = lax.axis_index("tensor") * segment + jnp.arange(segment)
    late = position >= half_len
    shift = jnp.stack([qv_bias[0], jnp.zeros_like(qv_bias[0]), qv_bias[1]])

    def hidden_of(index):
        embedded = sinusoid(timesteps[index], width)
        temb = jnp.where(late[:, None, None], embedded[None, :, 1], embedded[None, :, 0])
        return tokens[index].astype(jnp.float32) + temb

    def gather(array):
        if cube:
            whole = gather_tokens(array.reshape(segment, width))
        else:
            whole = lax.all_gather(array, "tensor", axis=0, tiled=True)
        return whole.reshape(seq_len, items_loc, width)

    def attention_of(whole):
        projected = jnp.einsum(
            "sid,kdc->kisc", whole, qkv_weight, preferred_element_type=jnp.float32
        )
        qkv = (projected + shift[:, None, None, :]).astype(low)
        context, logsum = attend(qkv, tile)
        return qkv, context, logsum

    hiddens = [hidden_of(index) for index in range(micro)]
    lows = [hidden.astype(low) for hidden in hiddens]
    out_flow = weight(out_weight, False)
    up_flow = weight(up_weight.T, False)
    down_flow = weight(down_weight, True)
    flows = (out_flow, up_flow, down_flow)
    gathered, kept = [], []
    for index in range(micro):
        if index < 2:
            for flow in flows:
                flow.step()
        whole = gate(flows, gather(lows[index]))
        if index < 2:
            for flow in flows:
                flow.step()
        gathered.append(whole)
        qkv, context, logsum = attention_of(whole)
        if index + 1 < micro:
            context, lows[index + 1] = gate(flows, context, lows[index + 1])
        kept.append((qkv, context, logsum))
    if cube:
        context_rows = tokens_of_heads(kept[0][1], kept[1][1])
    else:
        context_rows = jnp.concatenate(
            [
                lax.all_to_all(
                    context.reshape(items_loc, parts, segment, columns), "tensor", 1, 1, tiled=True
                )
                .transpose(2, 0, 1, 3)
                .reshape(segment * items_loc, parts * columns)
                for _, context, _ in kept
            ],
            axis=0,
        )
    context_rows = gate(flows, context_rows)
    for flow in flows:
        flow.step()
    bias_all = up_bias[None]
    if cube:
        for bit in (4, 2, 1):
            bias_all = jnp.concatenate([bias_all, swap_t(bias_all, bit)], axis=0)
    else:
        bias_all = lax.all_gather(up_bias, "tensor", axis=0, tiled=False)
    bias_all = bias_all.reshape(1, -1)
    out_all, up_all, down_all = out_flow.matrix(), up_flow.matrix(), down_flow.matrix()

    rows = micro * segment * items_loc
    hidden = jnp.stack(hiddens).reshape(rows, width)
    attention = mm(context_rows, out_all, ((1,), (0,)))
    normed, unit_one, inverse_one = norm_forward(
        hidden + (attention + out_bias), norm1_gain, norm1_bias
    )
    normed_low = normed.astype(low)
    pre = mm(normed_low, up_all, ((1,), (1,))) + bias_all
    half_gate = 0.5 * (1.0 + lax.erf(pre * INV_ROOT_TWO))
    act_low = (pre * half_gate).astype(low)
    slope = half_gate + pre * jnp.exp(-0.5 * pre * pre) * INV_ROOT_TWO_PI
    branch = mm(act_low, down_all, ((1,), (0,)))
    result, unit_two, inverse_two = norm_forward(
        normed + (branch + down_bias), norm2_gain, norm2_bias
    )
    layer_out = result.astype(low).reshape(tokens.shape)

    count_f = counts.astype(jnp.float32)
    total = jnp.sum(count_f).reshape(1, 1)
    if cube:
        for bit in (1, 2):
            total = total + swap_dp(total, bit)
    else:
        total = lax.psum(total, "dp")
    item_weight = count_f * float(micro * items_loc * replicas) / total
    keep = jnp.where(late[None, :, None], bucket[:, None, :], 1).astype(jnp.float32)
    factor = (keep * item_weight[:, None, :]).reshape(rows, 1)
    grad_out = cotangent.astype(jnp.float32).reshape(rows, width) * factor
    gain_two_grad = jnp.sum(grad_out * unit_two, axis=0)
    shift_two_grad = jnp.sum(grad_out, axis=0)
    grad_sum = norm_backward(grad_out, unit_two, inverse_two, norm2_gain)
    down_bias_grad = jnp.sum(grad_sum, axis=0)
    grad_sum_low = grad_sum.astype(low)

    down_grad = weight_grad(act_low, pick(grad_sum_low), True)
    if cube:
        grad_sum_low, down_grad.sent = lax.optimization_barrier((grad_sum_low, down_grad.sent))
    grad_act = mm(grad_sum_low, down_all, ((1,), (1,)))
    grad_pre = (grad_act * slope).astype(low)
    up_bias_grad = jnp.sum(grad_pre, axis=0, dtype=jnp.float32).reshape(parts, -1)
    up_grad = weight_grad(grad_pre, pick(normed_low), False)
    down_grad.join()
    grad_pre = gate((down_grad,), grad_pre)
    down_grad.step()
    grad_normed = grad_sum + mm(grad_pre, up_all, ((1,), (0,)))
    up_grad.join()
    grad_normed = gate((up_grad,), grad_normed)
    up_grad.step()
    gain_one_grad = jnp.sum(grad_normed * unit_one, axis=0)
    shift_one_grad = jnp.sum(grad_normed, axis=0)
    grad_mixed = norm_backward(grad_normed, unit_one, inverse_one, norm1_gain)
    out_bias_grad = jnp.sum(grad_mixed, axis=0)
    grad_mixed_low = grad_mixed.astype(low)
    vector_total = jnp.stack(
        [
            out_bias_grad,
            gain_one_grad,
            shift_one_grad,
            down_bias_grad,
            gain_two_grad,
            shift_two_grad,
        ]
    )
    grad_context = mm(grad_mixed_low, out_all, ((1,), (1,))).astype(low)
    out_grad = weight_grad(context_rows, pick(grad_mixed_low), True)
    out_grad.join()
    grad_context = gate((out_grad,), grad_context)
    out_grad.step()

    if cube:
        grad_heads = list(heads_of_tokens(grad_context))
    else:
        grad_heads = [
            lax.all_to_all(
                grad_context.reshape(micro, segment, items_loc, parts, columns)[index].transpose(
                    2, 1, 0, 3
                ),
                "tensor",
                0,
                0,
                tiled=True,
            )
            .transpose(1, 0, 2, 3)
            .reshape(items_loc, seq_len, columns)
            for index in range(micro)
        ]
    flows = (down_grad, up_grad, out_grad)
    qkv_total, bias_total, input_grads = None, None, []
    for index in range(micro):
        qkv, context, logsum = kept[index]
        grad_stack = attend_back(qkv, context, logsum, grad_heads[index], tile)
        bias_grad = jnp.stack(
            [
                jnp.sum(grad_stack[0], axis=(0, 1), dtype=jnp.float32),
                jnp.sum(grad_stack[2], axis=(0, 1), dtype=jnp.float32),
            ]
        )
        partial = jnp.einsum(
            "kisc,kdc->sid", grad_stack, qkv_weight, preferred_element_type=jnp.float32
        ).astype(low)
        if index < 2:
            partial = gate(flows, partial)
            for flow in flows:
                flow.step()
        if cube:
            summed = scatter_tokens(partial.reshape(parts, segment, width))
            if index + 1 < micro:
                grad_heads[index + 1], summed = lax.optimization_barrier(
                    (grad_heads[index + 1], summed)
                )
            else:
                summed = gate(flows, summed)
                for flow in flows:
                    flow.step()
        else:
            summed = lax.psum_scatter(partial, "tensor", scatter_dimension=0, tiled=True)
        input_grads.append(summed.astype(jnp.float32).reshape(segment, items_loc, width))
        qkv_part = jnp.einsum(
            "sid,kisc->kdc", gathered[index], grad_stack, preferred_element_type=jnp.float32
        )
        qkv_total = qkv_part if qkv_total is None else qkv_total + qkv_part
        bias_total = bias_grad if bias_total is None else bias_total + bias_grad
    qkv_total = qkv_total.astype(low)
    if cube:
        qkv_grad = scatter_qkv(qkv_total)
        for bit in (1, 2):
            bias_total = bias_total + swap_dp(bias_total, bit)
        size = columns // 4
        qv_bias_grad = lax.dynamic_slice_in_dim(bias_total, lax.axis_index("dp") * size, size, 1)
        vector_grads, up_bias_grad = sum_small(vector_total, up_bias_grad)
    else:
        qkv_grad = lax.psum_scatter(qkv_total, "dp", scatter_dimension=1, tiled=True)
        qv_bias_grad = lax.psum_scatter(bias_total, "dp", scatter_dimension=1, tiled=True)
        vector_grads = lax.psum_scatter(
            vector_total, ("dp", "tensor"), scatter_dimension=1, tiled=True
        )
        up_bias_grad = lax.psum_scatter(
            up_bias_grad, "tensor", scatter_dimension=0, tiled=True
        )[0]
        up_bias_grad = lax.psum_scatter(up_bias_grad, "dp", scatter_dimension=0, tiled=True)
    tokens_grad = grad_mixed.reshape(tokens.shape) + jnp.stack(input_grads)
    return (
        layer_out,
        tokens_grad,
        qkv_grad.astype(jnp.float32),
        qv_bias_grad,
        out_grad.shard().astype(jnp.float32),
        up_grad.shard().astype(jnp.float32).T,
        up_bias_grad,
        down_grad.shard().astype(jnp.float32),
        vector_grads,
    )


def solution(mesh):
    placed = (
        P(None, "tensor", "dp", None),
        P(None, "tensor", "dp", None),
        P(None, "dp", None),
        P(None, "dp"),
        P(None, "dp"),
        P(None, None, "tensor"),
        P(None, "tensor"),
        P("tensor", None),
        P(),
        P(),
        P(),
        P(None, "tensor"),
        P("tensor"),
        P("tensor", None),
        P(),
        P(),
        P(),
    )
    return jax.shard_map(
        body,
        mesh=mesh,
        in_specs=placed,
        out_specs=(
            P(None, "tensor", "dp", None),
            P(None, "tensor", "dp", None),
            P(None, "dp", "tensor"),
            P(None, ("tensor", "dp")),
            P("tensor", "dp"),
            P("dp", "tensor"),
            P(("tensor", "dp")),
            P("tensor", "dp"),
            P(None, ("dp", "tensor")),
        ),
        check_vma=False,
    )
```
